32 devices in a mesh: shot: 2 (over y), gx: 4 (over x, core), gy: 4 (over z).
Axes of the slice: x: 2, y: 2, z: 4, core: 2. Of those that a mesh axis runs over, the one named last changes fastest.
Arguments:
- src_p_prev: float32 [128, 64, 128], P(('shot', 'gx'), 'gy'), parts along dimension 0, may hold values from -6 to 6
- src_p_now: float32 [128, 64, 128], P(('shot', 'gx'), 'gy'), parts along dimension 0, may hold values from -6 to 6
- src_q_prev: float32 [128, 64, 128], P(('shot', 'gx'), 'gy'), parts along dimension 0, may hold values from -6 to 6
- src_q_now: float32 [128, 64, 128], P(('shot', 'gx'), 'gy'), parts along dimension 0, may hold values from -6 to 6
- rec_p_next: float32 [128, 64, 128], P(('shot', 'gx'), 'gy'), parts along dimension 0, may hold values from -6 to 6
- rec_p_now: float32 [128, 64, 128], P(('shot', 'gx'), 'gy'), parts along dimension 0, may hold values from -6 to 6
- rec_q_next: float32 [128, 64, 128], P(('shot', 'gx'), 'gy'), parts along dimension 0, may hold values from -6 to 6
- rec_q_now: float32 [128, 64, 128], P(('shot', 'gx'), 'gy'), parts along dimension 0, may hold values from -6 to 6
- velocity_term: float32 [64, 64, 128], P('gx', 'gy'), may hold values from 0.12 to 0.16
- epsilon: float32 [64, 64, 128], P('gx', 'gy'), may hold values from 0.2 to 0.4
- delta: float32 [64, 64, 128], P('gx', 'gy'), may hold values from 0 to 0.2
- tilt: float32 [64, 64, 128], P('gx', 'gy'), may hold values from 0 to 1.2
- azimuth: float32 [64, 64, 128], P('gx', 'gy'), may hold values from -3.140625 to 3.140625
- traces: float32 [32, 1024], P('shot', ('gx', 'gy')), parts along dimension 0, may hold values from -6 to 6
- receiver_x: int32 [1024], replicated, may hold values from 0 to 63
- receiver_y: int32 [1024], replicated, may hold values from 0 to 63
- segment_start: int32 [1], replicated, may hold values from 0 to 12
Outputs:
- image: float32 [128, 64, 128], P(('shot', 'gx'), 'gy'), parts along dimension 0
- rec_p_last: float32 [128, 64, 128], P(('shot', 'gx'), 'gy'), parts along dimension 0
- rec_q_last: float32 [128, 64, 128], P(('shot', 'gx'), 'gy'), parts along dimension 0
The draws below stay inside these ranges and needn't reach their ends.
There are 2 independent parts, one for each index of `shot`. The reference program is written for one: setup_inputs(seed, part) draws one part's arguments, and reference() takes and returns one part's arrays. A program takes and returns all parts, laid end to end along the dimension named above; an argument that names none is the same for every part. Nothing has to cross between parts.
All inputs are finite; a program needn't handle non-finite values.
Results may differ from the reference program's by a relative error of at most 0.00021.
Values sent between devices are 32-bit elements; how exact they have to be, the bound alone decides.
A program may use at most 64 MiB of HBM per device.

```python
import jax
import jax.numpy as jnp
from jax import lax

NZ = 128
STEPS = 4
NT = 16
REC_DEPTH = 4
NX = 64
NY = 64
NREC = 1024


def checker_field(key, salt):
    field_key = jax.random.fold_in(key, salt)
    noise_key = jax.random.fold_in(field_key, 0)
    row_index = lax.broadcasted_iota(jnp.int32, (NX, NY, NZ), 0)
    col_index = lax.broadcasted_iota(jnp.int32, (NX, NY, NZ), 1)
    sign_pattern = (1 - 2 * ((row_index + col_index) % 2)).astype(jnp.float32)
    noise = jax.random.normal(noise_key, (NX, NY, NZ), jnp.float32)
    amplitude = 1.0 + 0.6 * noise
    return jnp.clip(sign_pattern * amplitude, -6.0, 6.0)


def draw_src_p_prev(key, part):
    return checker_field(key, 101)


def draw_src_p_now(key, part):
    return checker_field(key, 102)


def draw_src_q_prev(key, part):
    return checker_field(key, 103)


def draw_src_q_now(key, part):
    return checker_field(key, 104)


def draw_rec_p_next(key, part):
    return checker_field(key, 105)


def draw_rec_p_now(key, part):
    return checker_field(key, 106)


def draw_rec_q_next(key, part):
    return checker_field(key, 107)


def draw_rec_q_now(key, part):
    return checker_field(key, 108)


def place_ends(result, stream_key, least, largest):
    place = [jax.random.randint(jax.random.fold_in(stream_key, axis), (), 0, length) for axis, length in enumerate(result.shape)]
    longest = result.shape.index(max(result.shape))
    neighbour = place[:longest] + [(place[longest] + 1) % result.shape[longest]] + place[longest + 1:]
    return result.at[tuple(place)].set(least).at[tuple(neighbour)].set(largest)


def levels(key, dims, pieces, least, high):
    gain, own = 1.0, jax.random.fold_in(key, 6)
    for position, parts in pieces:
        steps = jnp.exp(jax.random.uniform(jax.random.fold_in(own, position), (parts,), jnp.float32, least / len(pieces), high / len(pieces)))
        gain = gain * jnp.repeat(steps, dims[position] // parts).reshape([-1 if axis == position else 1 for axis in range(len(dims))])
    return gain


def gaussian(stream_key, shape, spread, limit, shards=(), held_as=jnp.bfloat16):
    drawn = jax.random.normal(stream_key, shape, jnp.float32) * spread
    if len(shards) > 0:
        drawn = levels(stream_key, shape, shards, -0.22, 0.18) * drawn
    return jnp.clip(drawn, min=-limit, max=limit).astype(held_as)


def setup_inputs(seed: int = 0, part: int = 0) -> dict:
    keys = jax.random.split(jax.random.key(seed), 18)
    own_keys = jax.random.split(jax.random.fold_in(keys[17], part), 18)
    src_p_prev = draw_src_p_prev(jax.random.fold_in(jax.random.fold_in(keys[17], part), 71), part)
    src_p_now = draw_src_p_now(jax.random.fold_in(jax.random.fold_in(keys[17], part), 71), part)
    src_q_prev = draw_src_q_prev(jax.random.fold_in(jax.random.fold_in(keys[17], part), 71), part)
    src_q_now = draw_src_q_now(jax.random.fold_in(jax.random.fold_in(keys[17], part), 71), part)
    rec_p_next = draw_rec_p_next(jax.random.fold_in(jax.random.fold_in(keys[17], part), 71), part)
    rec_p_now = draw_rec_p_now(jax.random.fold_in(jax.random.fold_in(keys[17], part), 71), part)
    rec_q_next = draw_rec_q_next(jax.random.fold_in(jax.random.fold_in(keys[17], part), 71), part)
    rec_q_now = draw_rec_q_now(jax.random.fold_in(jax.random.fold_in(keys[17], part), 71), part)
    velocity_term = jnp.clip(0.12 + 0.04 * jax.random.uniform(keys[8], (NX, NY, NZ), jnp.float32) ** levels(keys[8], (NX, NY, NZ), ((0, 4), (1, 4)), -0.2, 0.2), 0.12, 0.16)
    epsilon = jnp.clip(0.2 + 0.2 * jax.random.uniform(keys[9], (NX, NY, NZ), jnp.float32) ** levels(keys[9], (NX, NY, NZ), ((0, 4), (1, 4)), -0.2, 0.2), 0.2, 0.4)
    delta = jnp.clip(0.2 * jax.random.uniform(keys[10], (NX, NY, NZ), jnp.float32) ** levels(keys[10], (NX, NY, NZ), ((0, 4), (1, 4)), -0.2, 0.2), 0.0, 0.2)
    tilt = jnp.clip(1.2 * jax.random.uniform(keys[11], (NX, NY, NZ), jnp.float32) ** levels(keys[11], (NX, NY, NZ), ((0, 4), (1, 4)), -0.2, 0.2), 0.0, 1.2)
    azimuth = jnp.clip(jax.random.uniform(keys[12], (NX, NY, NZ), jnp.float32, -3.140625, 3.140625), -3.140625, 3.140625)
    traces = gaussian(own_keys[13], (NT, NREC), 1.0, 6.0, ((1, 16),), jnp.float32)
    receiver_x = place_ends(jax.random.randint(keys[14], (NREC,), 0, NX), jax.random.fold_in(keys[14], 1), 0, NX - 1).astype(jnp.int32)
    receiver_y = place_ends(jax.random.randint(keys[15], (NREC,), 0, NY), jax.random.fold_in(keys[15], 1), 0, NY - 1).astype(jnp.int32)
    segment_start = jax.random.randint(keys[16], (1,), 0, NT - STEPS + 1).astype(jnp.int32)
    return dict(src_p_prev=src_p_prev, src_p_now=src_p_now, src_q_prev=src_q_prev, src_q_now=src_q_now, rec_p_next=rec_p_next, rec_p_now=rec_p_now, rec_q_next=rec_q_next, rec_q_now=rec_q_now, velocity_term=velocity_term, epsilon=epsilon, delta=delta, tilt=tilt, azimuth=azimuth, traces=traces, receiver_x=receiver_x, receiver_y=receiver_y, segment_start=segment_start)


def factors_of(velocity_term, epsilon, delta, tilt, azimuth):
    sin_tilt = jnp.sin(tilt)
    cos_tilt = jnp.cos(tilt)
    sin_azim = jnp.sin(azimuth)
    cos_azim = jnp.cos(azimuth)
    sin_square = sin_tilt * sin_tilt
    double_tilt = 2.0 * sin_tilt * cos_tilt
    return (velocity_term, 1.0 + 2.0 * epsilon, jnp.sqrt(1.0 + 2.0 * delta), sin_square * cos_azim * cos_azim, sin_square * sin_azim * sin_azim, cos_tilt * cos_tilt, 2.0 * sin_square * sin_azim * cos_azim, double_tilt * cos_azim, double_tilt * sin_azim)

def rotated(padded, factors):
    center = padded[1:-1, 1:-1, 1:-1]
    d_xx = padded[2:, 1:-1, 1:-1] - 2.0 * center + padded[:-2, 1:-1, 1:-1]
    d_yy = padded[1:-1, 2:, 1:-1] - 2.0 * center + padded[1:-1, :-2, 1:-1]
    d_zz = padded[1:-1, 1:-1, 2:] - 2.0 * center + padded[1:-1, 1:-1, :-2]
    d_xy = 0.25 * (padded[2:, 2:, 1:-1] - padded[2:, :-2, 1:-1] - padded[:-2, 2:, 1:-1] + padded[:-2, :-2, 1:-1])
    d_xz = 0.25 * (padded[2:, 1:-1, 2:] - padded[2:, 1:-1, :-2] - padded[:-2, 1:-1, 2:] + padded[:-2, 1:-1, :-2])
    d_yz = 0.25 * (padded[1:-1, 2:, 2:] - padded[1:-1, 2:, :-2] - padded[1:-1, :-2, 2:] + padded[1:-1, :-2, :-2])
    along_axis = factors[3] * d_xx + factors[4] * d_yy + factors[5] * d_zz + factors[6] * d_xy + factors[7] * d_xz + factors[8] * d_yz
    return (along_axis, d_xx + d_yy + d_zz)

def advance(wave_state, factors):
    p_prev, p_now, q_prev, q_now = wave_state
    p_axis, p_laplace = rotated(jnp.pad(p_now, 1), factors)
    q_axis = rotated(jnp.pad(q_now, 1), factors)[0]
    p_across = p_laplace - p_axis
    p_next = 2.0 * p_now - p_prev + factors[0] * (factors[1] * p_across + factors[2] * q_axis)
    q_next = 2.0 * q_now - q_prev + factors[0] * (factors[2] * p_across + q_axis)
    return (p_next, q_next)

def reference(src_p_prev, src_p_now, src_q_prev, src_q_now, rec_p_next, rec_p_now, rec_q_next, rec_q_now, velocity_term, epsilon, delta, tilt, azimuth, traces, receiver_x, receiver_y, segment_start):
    factors = factors_of(velocity_term, epsilon, delta, tilt, azimuth)
    source_snaps = [src_p_now]
    wave_state = (src_p_prev, src_p_now, src_q_prev, src_q_now)
    for turn_index in range(STEPS):
        p_next, q_next = advance(wave_state, factors)
        wave_state = (wave_state[1], p_next, wave_state[3], q_next)
        source_snaps.append(p_next)
    window = lax.dynamic_slice_in_dim(traces, segment_start[0], STEPS, 0)
    image_sum = source_snaps[STEPS] * rec_p_now
    wave_state = (rec_p_next, rec_p_now, rec_q_next, rec_q_now)
    for turn_index in range(STEPS):
        sample = STEPS - 1 - turn_index
        p_next, q_next = advance(wave_state, factors)
        planes = jnp.zeros((NX, NY), jnp.float32).at[receiver_x, receiver_y].add(window[sample])
        p_next = p_next.at[:, :, REC_DEPTH].add(planes)
        wave_state = (wave_state[1], p_next, wave_state[3], q_next)
        image_sum = image_sum + source_snaps[sample] * p_next
    return (image_sum, wave_state[1], wave_state[3])
```

```python
import functools

import jax
import jax.numpy as jnp
from jax import lax
from jax.experimental import pallas as pl
from jax.experimental.pallas import tpu as pltpu
from jax.sharding import PartitionSpec as P

STEPS = 4
REC_DEPTH = 4
TOP = 8
LANES = 128
DIRS = tuple((dx, dy) for dx in (-1, 0, 1) for dy in (-1, 0, 1) if (dx, dy) != (0, 0))
DIRS = tuple(sorted(DIRS, key=lambda d: abs(d[0]) + abs(d[1])))
MESH = pl.DeviceIdType.MESH


def sine(x):
    s = x * x
    c = 1.6059044e-10
    for k in (-2.5052108e-8, 2.7557319e-6, -1.98412698e-4, 8.3333333e-3, -1.66666667e-1):
        c = c * s + k
    return x + x * (s * c)


def cosine(x):
    s = x * x
    c = -1.1470746e-11
    for k in (2.0876757e-9, -2.7557319e-7, 2.4801587e-5, -1.38888889e-3, 4.16666667e-2, -0.5):
        c = c * s + k
    return 1.0 + s * c


def kernel(sizes, *refs):
    n_gx, n_gy, nx, ny, nz, local_rec, n_rec = sizes
    fields, model = refs[:8], refs[8:13]
    traces, rec_x, rec_y, start = refs[13:17]
    image, p_last, q_last = refs[17:20]
    (waves, olds, coef, earth, inject, rows, window, gathered, rec_pos,
     load_sem, send_sem, recv_sem, far_send, far_recv) = refs[20:]
    n = n_gx * n_gy
    gx, gy = lax.axis_index("gx"), lax.axis_index("gy")
    me = gx * n_gy + gy

    barrier = pltpu.get_barrier_semaphore()

    def peer_id(i):
        peer = lax.rem(me + i, n)
        return {"gx": peer // n_gy, "gy": lax.rem(peer, n_gy)}

    def greet(i, carry):
        pl.semaphore_signal(barrier, inc=1, device_id=peer_id(i), device_id_type=MESH)
        return carry

    lax.fori_loop(1, n, greet, 0)

    inner_x, inner_y = pl.ds(1, nx), pl.ds(TOP, ny)
    loads = {}

    def load(name, src, dst):
        copy = pltpu.make_async_copy(src, dst, load_sem.at[len(loads)])
        copy.start()
        loads[name] = copy

    load("traces", traces, rows)
    for g in range(2):
        for f in range(2):
            load(("now", g, f), fields[4 * g + 2 * f + 1], waves.at[g, 0, f, inner_x, inner_y])
    for i in range(5):
        load(("model", i), model[i], earth.at[i])
    for g in range(2):
        for f in range(2):
            load(("prev", g, f), fields[4 * g + 2 * f], olds.at[g, f])
    load("rx", rec_x, rec_pos.at[0])
    load("ry", rec_y, rec_pos.at[1])

    for edge, plane in ((gx == 0, 0), (gx == n_gx - 1, nx + 1)):
        @pl.when(edge)
        def _():
            for g in range(2):
                for level in range(STEPS):
                    for f in range(2):
                        waves[g, level, f, plane, TOP - 8:TOP + ny + 8] = jnp.zeros((ny + 16, nz), jnp.float32)
    for edge, row in ((gy == 0, TOP - 1), (gy == n_gy - 1, TOP + ny)):
        @pl.when(edge)
        def _():
            for g in range(2):
                for level in range(STEPS):
                    for f in range(2):
                        waves[g, level, f, :, row:row + 1] = jnp.zeros((nx + 2, 1, nz), jnp.float32)

    loads["traces"].wait()
    window[...] = jnp.zeros_like(window)
    window[0:STEPS, 0:local_rec] = rows[pl.ds(start[0], STEPS), :]

    def there(dx, dy):
        ok = None
        for d, pos, count in ((dx, gx, n_gx), (dy, gy, n_gy)):
            if d:
                test = pos + d < count if d > 0 else pos + d >= 0
                ok = test if ok is None else ok & test
        return ok

    def halo_copy(g, level, i):
        dx, dy = DIRS[i]
        src_x = {0: inner_x, 1: pl.ds(nx, 1), -1: pl.ds(1, 1)}[dx]
        dst_x = {0: inner_x, 1: pl.ds(0, 1), -1: pl.ds(nx + 1, 1)}[dx]
        src_y = {0: inner_y, 1: pl.ds(TOP + ny - 1, 1), -1: pl.ds(TOP, 1)}[dy]
        dst_y = {0: inner_y, 1: pl.ds(TOP - 1, 1), -1: pl.ds(TOP + ny, 1)}[dy]
        return pltpu.make_async_remote_copy(
            src_ref=waves.at[g, level, :, src_x, src_y],
            dst_ref=waves.at[g, level, :, dst_x, dst_y],
            send_sem=send_sem.at[g, level, i],
            recv_sem=recv_sem.at[g, level, i],
            device_id={"gx": gx + dx, "gy": gy + dy},
            device_id_type=MESH,
        )

    def send_halo(g, level):
        for i, (dx, dy) in enumerate(DIRS):
            @pl.when(there(dx, dy))
            def _():
                halo_copy(g, level, i).start()

    def await_halo(g, level):
        for i, (dx, dy) in enumerate(DIRS):
            @pl.when(there(-dx, -dy))
            def _():
                halo_copy(g, level, i).wait_recv()

    def finish_halo(g, level):
        for i, (dx, dy) in enumerate(DIRS):
            @pl.when(there(dx, dy))
            def _():
                halo_copy(g, level, i).wait_send()

    def far_copy(i):
        return pltpu.make_async_remote_copy(
            src_ref=window,
            dst_ref=gathered.at[me],
            send_sem=far_send.at[i],
            recv_sem=far_recv.at[me],
            device_id=peer_id(i),
            device_id_type=MESH,
        )

    def far_start(i, carry):
        far_copy(i).start()
        return carry

    def far_finish(i, carry):
        far_copy(i).wait_send()
        return carry

    def far_await(i, carry):
        peer = lax.rem(me + i, n)
        pltpu.make_async_remote_copy(
            src_ref=window,
            dst_ref=gathered.at[peer],
            send_sem=far_send.at[i],
            recv_sem=far_recv.at[peer],
            device_id=peer_id(i),
            device_id_type=MESH,
        ).wait_recv()
        return carry

    for g in range(2):
        for f in range(2):
            loads["now", g, f].wait()
    gathered[me] = window[...]
    pl.semaphore_wait(barrier, n - 1)
    send_halo(0, 0)
    lax.fori_loop(1, n, far_start, 0)
    send_halo(1, 0)

    for i in range(5):
        loads["model", i].wait()

    def factors(x, carry):
        v = earth[0, x]
        f_e = 1.0 + 2.0 * earth[1, x]
        f_d = jnp.sqrt(1.0 + 2.0 * earth[2, x])
        tilt = earth[3, x]
        half = 0.5 * earth[4, x]
        sin_t, cos_t = sine(tilt), cosine(tilt)
        sin_h, cos_h = sine(half), cosine(half)
        sin_a = 2.0 * sin_h * cos_h
        cos_a = 1.0 - 2.0 * sin_h * sin_h
        square = sin_t * sin_t
        twice = (0.5 * sin_t) * cos_t
        coef[0, x] = square * cos_a * cos_a
        coef[1, x] = square * sin_a * sin_a
        coef[2, x] = cos_t * cos_t
        coef[3, x] = (0.5 * square) * sin_a * cos_a
        coef[4, x] = twice * cos_a
        coef[5, x] = twice * sin_a
        coef[6, x] = v * f_e
        coef[7, x] = v * f_d
        return carry

    lax.fori_loop(0, nx, factors, 0, unroll=2)

    for g in range(2):
        for f in range(2):
            loads["prev", g, f].wait()
    loads["rx"].wait()
    loads["ry"].wait()

    lane = lax.broadcasted_iota(jnp.int32, (ny, nz), 1)
    first, last = lane == 0, lane == nz - 1

    def after(value):
        return jnp.where(last, 0.0, pltpu.roll(value, nz - 1, 1))

    def before(value):
        return jnp.where(first, 0.0, pltpu.roll(value, 1, 1))

    mid, up, down = pl.ds(TOP, ny), pl.ds(TOP + 1, ny), pl.ds(TOP - 1, ny)

    def rotated(now, f, x):
        center = now[f, x + 1, mid]
        x_up, x_down = now[f, x + 2, mid], now[f, x, mid]
        y_up, y_down = now[f, x + 1, up], now[f, x + 1, down]
        d_x, d_y = x_up - x_down, y_up - y_down
        s_x, s_y = x_up + x_down, y_up + y_down
        s_z = after(center) + before(center)
        d_xy = (now[f, x + 2, up] - now[f, x + 2, down]) - (now[f, x, up] - now[f, x, down])
        d_xz = after(d_x) - before(d_x)
        d_yz = after(d_y) - before(d_y)
        axis = (
            (coef[0, x] * s_x + coef[1, x] * s_y)
            + (coef[2, x] * s_z + coef[3, x] * d_xy)
            + (coef[4, x] * d_xz + coef[5, x] * d_yz)
        ) - 2.0 * center
        return center, axis, (s_x + s_y) + (s_z - 6.0 * center)

    def step(g, level):
        now = waves.at[g, level]

        def plane(x, carry):
            p_now, p_axis, laplace = rotated(now, 0, x)
            q_now, q_axis, _ = rotated(now, 1, x)
            across = laplace - p_axis
            if level == 0:
                p_prev, q_prev = olds[g, 0, x], olds[g, 1, x]
            else:
                p_prev, q_prev = waves[g, level - 1, 0, x + 1, mid], waves[g, level - 1, 1, x + 1, mid]
            v_d = coef[7, x]
            p_next = (2.0 * p_now - p_prev) + (coef[6, x] * across + v_d * q_axis)
            q_next = (2.0 * q_now - q_prev) + (v_d * across + earth[0, x] * q_axis)
            if g == 1:
                p_next = p_next + inject[STEPS - 1 - level, x]
            if g == 1 and level == STEPS - 1:
                p_last[x] = p_next
                q_last[x] = q_next
                total = waves[0, 0, 0, x + 1, mid] * p_next
                for k in range(STEPS):
                    total = total + waves[1, k, 0, x + 1, mid] * waves[0, STEPS - k, 0, x + 1, mid]
                image[x] = total
            else:
                waves[g, level + 1, 0, x + 1, mid] = p_next
                waves[g, level + 1, 1, x + 1, mid] = q_next
            return carry

        lax.fori_loop(0, nx, plane, 0, unroll=2)

    def make_planes():
        per_row = LANES // local_rec
        n_rows = n_rec // LANES
        chunk = min(8, n_rows)
        x_id = lax.broadcasted_iota(jnp.int32, (nx, LANES), 0) + gx * nx
        y_id = lax.broadcasted_iota(jnp.int32, (ny, LANES), 0) + gy * ny
        total = jnp.zeros((ny, STEPS * nx), jnp.float32)
        for base in range(0, n_rows, chunk):
            lefts, rights = [], []
            for i in range(base, base + chunk):
                sample = gathered[i * per_row]
                for j in range(1, per_row):
                    sample = sample + pltpu.roll(gathered[i * per_row + j], j * local_rec, 1)
                at_x = rec_pos[0, i:i + 1] == x_id
                lefts.append(jnp.where(rec_pos[1, i:i + 1] == y_id, 1.0, 0.0))
                rights.append(
                    jnp.concatenate(
                        [jnp.where(at_x, sample[k:k + 1], 0.0) for k in range(STEPS)], axis=0
                    )
                )
            total = total + lax.dot_general(
                jnp.concatenate(lefts, axis=1),
                jnp.concatenate(rights, axis=1),
                (((1,), (1,)), ((), ())),
                precision=lax.Precision.HIGHEST,
                preferred_element_type=jnp.float32,
            )
        here = lane == REC_DEPTH
        for k in range(STEPS):
            for x in range(nx):
                column = k * nx + x
                inject[k, x] = jnp.where(here, total[:, column:column + 1], 0.0)

    for level in range(STEPS):
        await_halo(0, level)
        step(0, level)
        if level < STEPS - 1:
            send_halo(0, level + 1)
        if level == 0:
            lax.fori_loop(1, n, far_await, 0)
            make_planes()
        await_halo(1, level)
        step(1, level)
        if level < STEPS - 1:
            send_halo(1, level + 1)
    lax.fori_loop(1, n, far_finish, 0)
    for level in range(STEPS):
        for g in range(2):
            finish_halo(g, level)


def per_device(*args):
    nx, ny, nz = args[0].shape
    n_gx, n_gy = lax.axis_size("gx"), lax.axis_size("gy")
    traces, receiver_x, receiver_y, segment_start = args[13:]
    samples, local_rec = traces.shape
    n_rec = receiver_x.shape[0]
    n = n_gx * n_gy
    sizes = (n_gx, n_gy, nx, ny, nz, local_rec, n_rec)
    positions = [r.reshape(n_rec // LANES, LANES) for r in (receiver_x, receiver_y)]
    anywhere = pl.BlockSpec(memory_space=pl.ANY)
    block = jax.ShapeDtypeStruct((nx, ny, nz), jnp.float32)
    return pl.pallas_call(
        functools.partial(kernel, sizes),
        out_shape=(block,) * 3,
        in_specs=[anywhere] * 16 + [pl.BlockSpec(memory_space=pltpu.SMEM)],
        out_specs=(pl.BlockSpec(memory_space=pltpu.VMEM),) * 3,
        scratch_shapes=[
            pltpu.VMEM((2, STEPS + 1, 2, nx + 2, ny + 16, nz), jnp.float32),
            pltpu.VMEM((2, 2, nx, ny, nz), jnp.float32),
            pltpu.VMEM((8, nx, ny, nz), jnp.float32),
            pltpu.VMEM((5, nx, ny, nz), jnp.float32),
            pltpu.VMEM((STEPS, nx, ny, nz), jnp.float32),
            pltpu.VMEM((samples, local_rec), jnp.float32),
            pltpu.VMEM((8, LANES), jnp.float32),
            pltpu.VMEM((n, 8, LANES), jnp.float32),
            pltpu.VMEM((2, n_rec // LANES, LANES), jnp.int32),
            pltpu.SemaphoreType.DMA((16,)),
            pltpu.SemaphoreType.DMA((2, STEPS, 8)),
            pltpu.SemaphoreType.DMA((2, STEPS, 8)),
            pltpu.SemaphoreType.DMA((n,)),
            pltpu.SemaphoreType.DMA((n,)),
        ],
        compiler_params=pltpu.CompilerParams(
            collective_id=0, has_side_effects=True, vmem_limit_bytes=48 * 1024 * 1024
        ),
        name="window",
    )(*args[:13], traces, *positions, segment_start)


def solution(mesh):
    block, cell = P(("shot", "gx"), "gy", None), P("gx", "gy", None)
    return jax.shard_map(
        per_device,
        mesh=mesh,
        in_specs=(block,) * 8 + (cell,) * 5 + (P("shot", ("gx", "gy")), P(), P(), P()),
        out_specs=(block,) * 3,
        check_vma=False,
    )
```

```python
import functools

import jax
import jax.numpy as jnp
from jax import lax
from jax.experimental import pallas as pl
from jax.experimental.pallas import tpu as pltpu
from jax.sharding import PartitionSpec as P

STEPS = 4
REC_DEPTH = 4
TOP = 8
LANES = 128
DIRS = tuple((dx, dy) for dx in (-1, 0, 1) for dy in (-1, 0, 1) if (dx, dy) != (0, 0))
DIRS = tuple(sorted(DIRS, key=lambda d: abs(d[0]) + abs(d[1])))
MESH = pl.DeviceIdType.MESH


def sine(x):
    s = x * x
    c = 1.6059044e-10
    for k in (-2.5052108e-8, 2.7557319e-6, -1.98412698e-4, 8.3333333e-3, -1.66666667e-1):
        c = c * s + k
    return x + x * (s * c)


def cosine(x):
    s = x * x
    c = -1.1470746e-11
    for k in (2.0876757e-9, -2.7557319e-7, 2.4801587e-5, -1.38888889e-3, 4.16666667e-2, -0.5):
        c = c * s + k
    return 1.0 + s * c


def kernel(sizes, *refs):
    n_gx, n_gy, nx, ny, nz, local_rec, n_rec = sizes
    fields, model = refs[:8], refs[8:13]
    traces, rec_x, rec_y, start = refs[13:17]
    image, p_last, q_last = refs[17:20]
    (waves, olds, coef, earth, inject, rows, window, gathered, rec_pos,
     load_sem, send_sem, recv_sem, far_send, far_recv) = refs[20:]
    n = n_gx * n_gy
    gx, gy = lax.axis_index("gx"), lax.axis_index("gy")
    me = gx * n_gy + gy

    barrier = pltpu.get_barrier_semaphore()

    def peer_id(i):
        peer = lax.rem(me + i, n)
        return {"gx": peer // n_gy, "gy": lax.rem(peer, n_gy)}

    def greet(i, carry):
        pl.semaphore_signal(barrier, inc=1, device_id=peer_id(i), device_id_type=MESH)
        return carry

    lax.fori_loop(1, n, greet, 0)

    inner_x, inner_y = pl.ds(1, nx), pl.ds(TOP, ny)
    loads = {}

    def load(name, src, dst):
        copy = pltpu.make_async_copy(src, dst, load_sem.at[len(loads)])
        copy.start()
        loads[name] = copy

    load("traces", traces, rows)
    for g in range(2):
        for f in range(2):
            load(("now", g, f), fields[4 * g + 2 * f + 1], waves.at[g, 0, f, inner_x, inner_y])
    for i in range(5):
        load(("model", i), model[i], earth.at[i])
    for g in range(2):
        for f in range(2):
            load(("prev", g, f), fields[4 * g + 2 * f], olds.at[g, f])
    load("rx", rec_x, rec_pos.at[0])
    load("ry", rec_y, rec_pos.at[1])

    for edge, plane in ((gx == 0, 0), (gx == n_gx - 1, nx + 1)):
        @pl.when(edge)
        def _():
            for g in range(2):
                for level in range(STEPS):
                    for f in range(2):
                        waves[g, level, f, plane, TOP - 8:TOP + ny + 8] = jnp.zeros((ny + 16, nz), jnp.float32)
    for edge, row in ((gy == 0, TOP - 1), (gy == n_gy - 1, TOP + ny)):
        @pl.when(edge)
        def _():
            for g in range(2):
                for level in range(STEPS):
                    for f in range(2):
                        waves[g, level, f, :, row:row + 1] = jnp.zeros((nx + 2, 1, nz), jnp.float32)

    loads["traces"].wait()
    window[...] = jnp.zeros_like(window)
    window[0:STEPS, 0:local_rec] = rows[pl.ds(start[0], STEPS), :]

    def there(dx, dy):
        ok = None
        for d, pos, count in ((dx, gx, n_gx), (dy, gy, n_gy)):
            if d:
                test = pos + d < count if d > 0 else pos + d >= 0
                ok = test if ok is None else ok & test
        return ok

    def halo_copy(g, level, i):
        dx, dy = DIRS[i]
        src_x = {0: inner_x, 1: pl.ds(nx, 1), -1: pl.ds(1, 1)}[dx]
        dst_x = {0: inner_x, 1: pl.ds(0, 1), -1: pl.ds(nx + 1, 1)}[dx]
        src_y = {0: inner_y, 1: pl.ds(TOP + ny - 1, 1), -1: pl.ds(TOP, 1)}[dy]
        dst_y = {0: inner_y, 1: pl.ds(TOP - 1, 1), -1: pl.ds(TOP + ny, 1)}[dy]
        return pltpu.make_async_remote_copy(
            src_ref=waves.at[g, level, :, src_x, src_y],
            dst_ref=waves.at[g, level, :, dst_x, dst_y],
            send_sem=send_sem.at[g, level, i],
            recv_sem=recv_sem.at[g, level, i],
            device_id={"gx": gx + dx, "gy": gy + dy},
            device_id_type=MESH,
        )

    def send_halo(g, level):
        for i, (dx, dy) in enumerate(DIRS):
            @pl.when(there(dx, dy))
            def _():
                halo_copy(g, level, i).start()

    def await_halo(g, level):
        for i, (dx, dy) in enumerate(DIRS):
            @pl.when(there(-dx, -dy))
            def _():
                halo_copy(g, level, i).wait_recv()

    def finish_halo(g, level):
        for i, (dx, dy) in enumerate(DIRS):
            @pl.when(there(dx, dy))
            def _():
                halo_copy(g, level, i).wait_send()

    def far_copy(i):
        return pltpu.make_async_remote_copy(
            src_ref=window,
            dst_ref=gathered.at[me],
            send_sem=far_send.at[i],
            recv_sem=far_recv.at[me],
            device_id=peer_id(i),
            device_id_type=MESH,
        )

    def far_start(i, carry):
        far_copy(i).start()
        return carry

    def far_finish(i, carry):
        far_copy(i).wait_send()
        return carry

    def far_await(i, carry):
        peer = lax.rem(me + i, n)
        pltpu.make_async_remote_copy(
            src_ref=window,
            dst_ref=gathered.at[peer],
            send_sem=far_send.at[i],
            recv_sem=far_recv.at[peer],
            device_id=peer_id(i),
            device_id_type=MESH,
        ).wait_recv()
        return carry

    for g in range(2):
        for f in range(2):
            loads["now", g, f].wait()
    gathered[me] = window[...]
    pl.semaphore_wait(barrier, n - 1)
    send_halo(0, 0)
    lax.fori_loop(1, n, far_start, 0)
    send_halo(1, 0)

    for i in range(5):
        loads["model", i].wait()

    def factors(x, carry):
        v = earth[0, x]
        f_e = 1.0 + 2.0 * earth[1, x]
        f_d = jnp.sqrt(1.0 + 2.0 * earth[2, x])
        tilt = earth[3, x]
        half = 0.5 * earth[4, x]
        sin_t, cos_t = sine(tilt), cosine(tilt)
        sin_h, cos_h = sine(half), cosine(half)
        sin_a = 2.0 * sin_h * cos_h
        cos_a = 1.0 - 2.0 * sin_h * sin_h
        square = sin_t * sin_t
        twice = (0.5 * sin_t) * cos_t
        coef[0, x] = square * cos_a * cos_a
        coef[1, x] = square * sin_a * sin_a
        coef[2, x] = cos_t * cos_t
        coef[3, x] = (0.5 * square) * sin_a * cos_a
        coef[4, x] = twice * cos_a
        coef[5, x] = twice * sin_a
        coef[6, x] = v * f_e
        coef[7, x] = v * f_d
        return carry

    lax.fori_loop(0, nx, factors, 0, unroll=2)

    for g in range(2):
        for f in range(2):
            loads["prev", g, f].wait()
    loads["rx"].wait()
    loads["ry"].wait()

    lane = lax.broadcasted_iota(jnp.int32, (ny, nz), 1)
    first, last = lane == 0, lane == nz - 1

    def after(value):
        return jnp.where(last, 0.0, pltpu.roll(value, nz - 1, 1))

    def before(value):
        return jnp.where(first, 0.0, pltpu.roll(value, 1, 1))

    mid, up, down = pl.ds(TOP, ny), pl.ds(TOP + 1, ny), pl.ds(TOP - 1, ny)

    def rotated(now, f, x):
        center = now[f, x + 1, mid]
        x_up, x_down = now[f, x + 2, mid], now[f, x, mid]
        y_up, y_down = now[f, x + 1, up], now[f, x + 1, down]
        d_x, d_y = x_up - x_down, y_up - y_down
        s_x, s_y = x_up + x_down, y_up + y_down
        s_z = after(center) + before(center)
        d_xy = (now[f, x + 2, up] - now[f, x + 2, down]) - (now[f, x, up] - now[f, x, down])
        d_xz = after(d_x) - before(d_x)
        d_yz = after(d_y) - before(d_y)
        axis = (
            (coef[0, x] * s_x + coef[1, x] * s_y)
            + (coef[2, x] * s_z + coef[3, x] * d_xy)
            + (coef[4, x] * d_xz + coef[5, x] * d_yz)
        ) - 2.0 * center
        return center, axis, (s_x + s_y) + (s_z - 6.0 * center)

    def step(g, level):
        now = waves.at[g, level]

        def plane(x, carry):
            p_now, p_axis, laplace = rotated(now, 0, x)
            q_now, q_axis, _ = rotated(now, 1, x)
            across = laplace - p_axis
            if level == 0:
                p_prev, q_prev = olds[g, 0, x], olds[g, 1, x]
            else:
                p_prev, q_prev = waves[g, level - 1, 0, x + 1, mid], waves[g, level - 1, 1, x + 1, mid]
            v_d = coef[7, x]
            p_next = (2.0 * p_now - p_prev) + (coef[6, x] * across + v_d * q_axis)
            q_next = (2.0 * q_now - q_prev) + (v_d * across + earth[0, x] * q_axis)
            if g == 1:
                p_next = p_next + inject[STEPS - 1 - level, x]
            if g == 1 and level == STEPS - 1:
                p_last[x] = p_next
                q_last[x] = q_next
                total = waves[0, 0, 0, x + 1, mid] * p_next
                for k in range(STEPS):
                    total = total + waves[1, k, 0, x + 1, mid] * waves[0, STEPS - k, 0, x + 1, mid]
                image[x] = total
            else:
                waves[g, level + 1, 0, x + 1, mid] = p_next
                waves[g, level + 1, 1, x + 1, mid] = q_next
            return carry

        lax.fori_loop(0, nx, plane, 0, unroll=2)

    def make_planes():
        per_row = LANES // local_rec
        n_rows = n_rec // LANES
        chunk = min(8, n_rows)
        x_id = lax.broadcasted_iota(jnp.int32, (nx, LANES), 0) + gx * nx
        y_id = lax.broadcasted_iota(jnp.int32, (ny, LANES), 0) + gy * ny
        total = jnp.zeros((ny, STEPS * nx), jnp.float32)
        for base in range(0, n_rows, chunk):
            lefts, rights = [], []
            for i in range(base, base + chunk):
                sample = gathered[i * per_row]
                for j in range(1, per_row):
                    sample = sample + pltpu.roll(gathered[i * per_row + j], j * local_rec, 1)
                at_x = rec_pos[0, i:i + 1] == x_id
                lefts.append(jnp.where(rec_pos[1, i:i + 1] == y_id, 1.0, 0.0))
                rights.append(
                    jnp.concatenate(
                        [jnp.where(at_x, sample[k:k + 1], 0.0) for k in range(STEPS)], axis=0
                    )
                )
            total = total + lax.dot_general(
                jnp.concatenate(lefts, axis=1),
                jnp.concatenate(rights, axis=1),
                (((1,), (1,)), ((), ())),
                precision=lax.Precision.HIGHEST,
                preferred_element_type=jnp.float32,
            )
        here = lane == REC_DEPTH
        for k in range(STEPS):
            for x in range(nx):
                column = k * nx + x
                inject[k, x] = jnp.where(here, total[:, column:column + 1], 0.0)

    for level in range(STEPS):
        await_halo(0, level)
        step(0, level)
        if level < STEPS - 1:
            send_halo(0, level + 1)
        if level == 0:
            lax.fori_loop(1, n, far_await, 0)
            make_planes()
        await_halo(1, level)
        step(1, level)
        if level < STEPS - 1:
            send_halo(1, level + 1)
    lax.fori_loop(1, n, far_finish, 0)
    for level in range(STEPS):
        for g in range(2):
            finish_halo(g, level)


def per_device(*args):
    nx, ny, nz = args[0].shape
    n_gx, n_gy = lax.axis_size("gx"), lax.axis_size("gy")
    traces, receiver_x, receiver_y, segment_start = args[13:]
    samples, local_rec = traces.shape
    n_rec = receiver_x.shape[0]
    n = n_gx * n_gy
    sizes = (n_gx, n_gy, nx, ny, nz, local_rec, n_rec)
    positions = [r.reshape(n_rec // LANES, LANES) for r in (receiver_x, receiver_y)]
    anywhere = pl.BlockSpec(memory_space=pltpu.HBM)
    block = jax.ShapeDtypeStruct((nx, ny, nz), jnp.float32)
    return pl.pallas_call(
        functools.partial(kernel, sizes),
        out_shape=(block,) * 3,
        in_specs=[anywhere] * 16 + [pl.BlockSpec(memory_space=pltpu.SMEM)],
        out_specs=(pl.BlockSpec(memory_space=pltpu.VMEM),) * 3,
        scratch_shapes=[
            pltpu.VMEM((2, STEPS + 1, 2, nx + 2, ny + 16, nz), jnp.float32),
            pltpu.VMEM((2, 2, nx, ny, nz), jnp.float32),
            pltpu.VMEM((8, nx, ny, nz), jnp.float32),
            pltpu.VMEM((5, nx, ny, nz), jnp.float32),
            pltpu.VMEM((STEPS, nx, ny, nz), jnp.float32),
            pltpu.VMEM((samples, local_rec), jnp.float32),
            pltpu.VMEM((8, LANES), jnp.float32),
            pltpu.VMEM((n, 8, LANES), jnp.float32),
            pltpu.VMEM((2, n_rec // LANES, LANES), jnp.int32),
            pltpu.SemaphoreType.DMA((16,)),
            pltpu.SemaphoreType.DMA((2, STEPS, 8)),
            pltpu.SemaphoreType.DMA((2, STEPS, 8)),
            pltpu.SemaphoreType.DMA((n,)),
            pltpu.SemaphoreType.DMA((n,)),
        ],
        compiler_params=pltpu.CompilerParams(
            collective_id=0, has_side_effects=True, vmem_limit_bytes=48 * 1024 * 1024
        ),
        name="window",
    )(*args[:13], traces, *positions, segment_start)


def solution(mesh):
    block, cell = P(("shot", "gx"), "gy", None), P("gx", "gy", None)
    return jax.shard_map(
        per_device,
        mesh=mesh,
        in_specs=(block,) * 8 + (cell,) * 5 + (P("shot", ("gx", "gy")), P(), P(), P()),
        out_specs=(block,) * 3,
        check_vma=False,
    )
```

```python
import functools

import jax
import jax.numpy as jnp
from jax import lax
from jax.experimental import pallas as pl
from jax.experimental.pallas import tpu as pltpu
from jax.sharding import PartitionSpec as P

STEPS = 4
REC_DEPTH = 4
TOP = 8
LANES = 128
DIRS = tuple((dx, dy) for dx in (-1, 0, 1) for dy in (-1, 0, 1) if (dx, dy) != (0, 0))
DIRS = tuple(sorted(DIRS, key=lambda d: abs(d[0]) + abs(d[1])))
MESH = pl.DeviceIdType.MESH


def sine(x):
    s = x * x
    c = 1.6059044e-10
    for k in (-2.5052108e-8, 2.7557319e-6, -1.98412698e-4, 8.3333333e-3, -1.66666667e-1):
        c = c * s + k
    return x + x * (s * c)


def cosine(x):
    s = x * x
    c = -1.1470746e-11
    for k in (2.0876757e-9, -2.7557319e-7, 2.4801587e-5, -1.38888889e-3, 4.16666667e-2, -0.5):
        c = c * s + k
    return 1.0 + s * c


def kernel(sizes, *refs):
    n_gx, n_gy, nx, ny, nz, local_rec, n_rec = sizes
    fields, model = refs[:8], refs[8:13]
    traces, rec_x, rec_y, start = refs[13:17]
    image, p_last, q_last = refs[17:20]
    (waves, olds, coef, earth, inject, rows, window, gathered, rec_pos,
     load_sem, send_sem, recv_sem, far_send, far_recv) = refs[20:]
    n = n_gx * n_gy
    gx, gy = lax.axis_index("gx"), lax.axis_index("gy")
    me = gx * n_gy + gy

    barrier = pltpu.get_barrier_semaphore()

    def peer_id(i):
        peer = lax.rem(me + i, n)
        return {"gx": peer // n_gy, "gy": lax.rem(peer, n_gy)}

    def greet(i, carry):
        pl.semaphore_signal(barrier, inc=1, device_id=peer_id(i), device_id_type=MESH)
        return carry

    lax.fori_loop(1, n, greet, 0)

    inner_x, inner_y = pl.ds(1, nx), pl.ds(TOP, ny)
    loads = {}

    def load(name, src, dst):
        copy = pltpu.make_async_copy(src, dst, load_sem.at[len(loads)])
        copy.start()
        loads[name] = copy

    load("traces", traces, rows)
    for g in range(2):
        for f in range(2):
            load(("now", g, f), fields[4 * g + 2 * f + 1], waves.at[g, 0, f, inner_x, inner_y])
    for i in range(5):
        load(("model", i), model[i], earth.at[i])
    for g in range(2):
        for f in range(2):
            load(("prev", g, f), fields[4 * g + 2 * f], olds.at[g, f])
    load("rx", rec_x, rec_pos.at[0])
    load("ry", rec_y, rec_pos.at[1])

    for edge, plane in ((gx == 0, 0), (gx == n_gx - 1, nx + 1)):
        @pl.when(edge)
        def _():
            for g in range(2):
                for level in range(STEPS):
                    for f in range(2):
                        waves[g, level, f, plane, TOP - 8:TOP + ny + 8] = jnp.zeros((ny + 16, nz), jnp.float32)
    for edge, row in ((gy == 0, TOP - 1), (gy == n_gy - 1, TOP + ny)):
        @pl.when(edge)
        def _():
            for g in range(2):
                for level in range(STEPS):
                    for f in range(2):
                        waves[g, level, f, :, row:row + 1] = jnp.zeros((nx + 2, 1, nz), jnp.float32)

    loads["traces"].wait()
    window[...] = jnp.zeros_like(window)
    window[0:STEPS, 0:local_rec] = rows[pl.ds(start[0], STEPS), :]

    def there(dx, dy):
        ok = None
        for d, pos, count in ((dx, gx, n_gx), (dy, gy, n_gy)):
            if d:
                test = pos + d < count if d > 0 else pos + d >= 0
                ok = test if ok is None else ok & test
        return ok

    def halo_copy(g, level, i):
        dx, dy = DIRS[i]
        src_x = {0: inner_x, 1: pl.ds(nx, 1), -1: pl.ds(1, 1)}[dx]
        dst_x = {0: inner_x, 1: pl.ds(0, 1), -1: pl.ds(nx + 1, 1)}[dx]
        src_y = {0: inner_y, 1: pl.ds(TOP + ny - 1, 1), -1: pl.ds(TOP, 1)}[dy]
        dst_y = {0: inner_y, 1: pl.ds(TOP - 1, 1), -1: pl.ds(TOP + ny, 1)}[dy]
        return pltpu.make_async_remote_copy(
            src_ref=waves.at[g, level, :, src_x, src_y],
            dst_ref=waves.at[g, level, :, dst_x, dst_y],
            send_sem=send_sem.at[g, level, i],
            recv_sem=recv_sem.at[g, level, i],
            device_id={"gx": gx + dx, "gy": gy + dy},
            device_id_type=MESH,
        )

    def send_halo(g, level):
        for i, (dx, dy) in enumerate(DIRS):
            @pl.when(there(dx, dy))
            def _():
                halo_copy(g, level, i).start()

    def await_halo(g, level):
        for i, (dx, dy) in enumerate(DIRS):
            @pl.when(there(-dx, -dy))
            def _():
                halo_copy(g, level, i).wait_recv()

    def finish_halo(g, level):
        for i, (dx, dy) in enumerate(DIRS):
            @pl.when(there(dx, dy))
            def _():
                halo_copy(g, level, i).wait_send()

    def far_copy(i):
        return pltpu.make_async_remote_copy(
            src_ref=window,
            dst_ref=gathered.at[me],
            send_sem=far_send.at[i],
            recv_sem=far_recv.at[me],
            device_id=peer_id(i),
            device_id_type=MESH,
        )

    def far_start(i, carry):
        far_copy(i).start()
        return carry

    def far_finish(i, carry):
        far_copy(i).wait_send()
        return carry

    def far_await(i, carry):
        peer = lax.rem(me + i, n)
        pltpu.make_async_remote_copy(
            src_ref=window,
            dst_ref=gathered.at[peer],
            send_sem=far_send.at[i],
            recv_sem=far_recv.at[peer],
            device_id=peer_id(i),
            device_id_type=MESH,
        ).wait_recv()
        return carry

    for g in range(2):
        for f in range(2):
            loads["now", g, f].wait()
    gathered[me] = window[...]
    pl.semaphore_wait(barrier, n - 1)
    send_halo(0, 0)
    lax.fori_loop(1, n, far_start, 0)
    send_halo(1, 0)

    for i in range(5):
        loads["model", i].wait()

    def factors(x, carry):
        v = earth[0, x]
        f_e = 1.0 + 2.0 * earth[1, x]
        f_d = jnp.sqrt(1.0 + 2.0 * earth[2, x])
        tilt = earth[3, x]
        half = 0.5 * earth[4, x]
        sin_t, cos_t = sine(tilt), cosine(tilt)
        sin_h, cos_h = sine(half), cosine(half)
        sin_a = 2.0 * sin_h * cos_h
        cos_a = 1.0 - 2.0 * sin_h * sin_h
        square = sin_t * sin_t
        twice = (0.5 * sin_t) * cos_t
        coef[0, x] = square * cos_a * cos_a
        coef[1, x] = square * sin_a * sin_a
        coef[2, x] = cos_t * cos_t
        coef[3, x] = (0.5 * square) * sin_a * cos_a
        coef[4, x] = twice * cos_a
        coef[5, x] = twice * sin_a
        coef[6, x] = v * f_e
        coef[7, x] = v * f_d
        return carry

    lax.fori_loop(0, nx, factors, 0, unroll=2)

    for g in range(2):
        for f in range(2):
            loads["prev", g, f].wait()
    loads["rx"].wait()
    loads["ry"].wait()

    lane = lax.broadcasted_iota(jnp.int32, (ny, nz), 1)
    first, last = lane == 0, lane == nz - 1

    def after(value):
        return jnp.where(last, 0.0, pltpu.roll(value, nz - 1, 1))

    def before(value):
        return jnp.where(first, 0.0, pltpu.roll(value, 1, 1))

    mid, up, down = pl.ds(TOP, ny), pl.ds(TOP + 1, ny), pl.ds(TOP - 1, ny)

    def rotated(now, f, x):
        center = now[f, x + 1, mid]
        x_up, x_down = now[f, x + 2, mid], now[f, x, mid]
        y_up, y_down = now[f, x + 1, up], now[f, x + 1, down]
        d_x, d_y = x_up - x_down, y_up - y_down
        s_x, s_y = x_up + x_down, y_up + y_down
        s_z = after(center) + before(center)
        d_xy = (now[f, x + 2, up] - now[f, x + 2, down]) - (now[f, x, up] - now[f, x, down])
        d_xz = after(d_x) - before(d_x)
        d_yz = after(d_y) - before(d_y)
        axis = (
            (coef[0, x] * s_x + coef[1, x] * s_y)
            + (coef[2, x] * s_z + coef[3, x] * d_xy)
            + (coef[4, x] * d_xz + coef[5, x] * d_yz)
        ) - 2.0 * center
        return center, axis, (s_x + s_y) + (s_z - 6.0 * center)

    def step(g, level):
        now = waves.at[g, level]

        def plane(x, carry):
            p_now, p_axis, laplace = rotated(now, 0, x)
            q_now, q_axis, _ = rotated(now, 1, x)
            across = laplace - p_axis
            if level == 0:
                p_prev, q_prev = olds[g, 0, x], olds[g, 1, x]
            else:
                p_prev, q_prev = waves[g, level - 1, 0, x + 1, mid], waves[g, level - 1, 1, x + 1, mid]
            v_d = coef[7, x]
            p_next = (2.0 * p_now - p_prev) + (coef[6, x] * across + v_d * q_axis)
            q_next = (2.0 * q_now - q_prev) + (v_d * across + earth[0, x] * q_axis)
            if g == 1:
                p_next = p_next + inject[STEPS - 1 - level, x]
            if g == 1 and level == STEPS - 1:
                p_last[x] = p_next
                q_last[x] = q_next
                total = waves[0, 0, 0, x + 1, mid] * p_next
                for k in range(STEPS):
                    total = total + waves[1, k, 0, x + 1, mid] * waves[0, STEPS - k, 0, x + 1, mid]
                image[x] = total
            else:
                waves[g, level + 1, 0, x + 1, mid] = p_next
                waves[g, level + 1, 1, x + 1, mid] = q_next
            return carry

        lax.fori_loop(0, nx, plane, 0, unroll=2)

    def make_planes():
        per_row = LANES // local_rec
        n_rows = n_rec // LANES
        chunk = min(8, n_rows)
        x_id = lax.broadcasted_iota(jnp.int32, (nx, LANES), 0) + gx * nx
        y_id = lax.broadcasted_iota(jnp.int32, (ny, LANES), 0) + gy * ny
        total = jnp.zeros((ny, STEPS * nx), jnp.float32)
        for base in range(0, n_rows, chunk):
            lefts, rights = [], []
            for i in range(base, base + chunk):
                sample = gathered[i * per_row]
                for j in range(1, per_row):
                    sample = sample + pltpu.roll(gathered[i * per_row + j], j * local_rec, 1)
                at_x = rec_pos[0, i:i + 1] == x_id
                lefts.append(jnp.where(rec_pos[1, i:i + 1] == y_id, 1.0, 0.0))
                rights.append(
                    jnp.concatenate(
                        [jnp.where(at_x, sample[k:k + 1], 0.0) for k in range(STEPS)], axis=0
                    )
                )
            total = total + lax.dot_general(
                jnp.concatenate(lefts, axis=1),
                jnp.concatenate(rights, axis=1),
                (((1,), (1,)), ((), ())),
                precision=lax.Precision.HIGHEST,
                preferred_element_type=jnp.float32,
            )
        here = lane == REC_DEPTH
        for k in range(STEPS):
            for x in range(nx):
                column = k * nx + x
                inject[k, x] = jnp.where(here, total[:, column:column + 1], 0.0)

    for level in range(STEPS):
        await_halo(0, level)
        step(0, level)
        if level < STEPS - 1:
            send_halo(0, level + 1)
        if level == 0:
            lax.fori_loop(1, n, far_await, 0)
            make_planes()
        await_halo(1, level)
        step(1, level)
        if level < STEPS - 1:
            send_halo(1, level + 1)
    lax.fori_loop(1, n, far_finish, 0)
    for level in range(STEPS):
        for g in range(2):
            finish_halo(g, level)


def per_device(*args):
    nx, ny, nz = args[0].shape
    n_gx, n_gy = lax.axis_size("gx"), lax.axis_size("gy")
    traces, receiver_x, receiver_y, segment_start = args[13:]
    samples, local_rec = traces.shape
    n_rec = receiver_x.shape[0]
    n = n_gx * n_gy
    sizes = (n_gx, n_gy, nx, ny, nz, local_rec, n_rec)
    positions = [r.reshape(n_rec // LANES, LANES) for r in (receiver_x, receiver_y)]
    anywhere = pl.BlockSpec(memory_space=pltpu.HBM)
    block = jax.ShapeDtypeStruct((nx, ny, nz), jnp.float32)
    return pl.pallas_call(
        functools.partial(kernel, sizes),
        out_shape=(block,) * 3,
        in_specs=[anywhere] * 16 + [pl.BlockSpec(memory_space=pltpu.SMEM)],
        out_specs=(pl.BlockSpec(memory_space=pltpu.VMEM),) * 3,
        scratch_shapes=[
            pltpu.VMEM((2, STEPS + 1, 2, nx + 2, ny + 16, nz), jnp.float32),
            pltpu.VMEM((2, 2, nx, ny, nz), jnp.float32),
            pltpu.VMEM((8, nx, ny, nz), jnp.float32),
            pltpu.VMEM((5, nx, ny, nz), jnp.float32),
            pltpu.VMEM((STEPS, nx, ny, nz), jnp.float32),
            pltpu.VMEM((samples, local_rec), jnp.float32),
            pltpu.VMEM((8, LANES), jnp.float32),
            pltpu.VMEM((n, 8, LANES), jnp.float32),
            pltpu.VMEM((2, n_rec // LANES, LANES), jnp.int32),
            pltpu.SemaphoreType.DMA((16,)),
            pltpu.SemaphoreType.DMA((2, STEPS, 8)),
            pltpu.SemaphoreType.DMA((2, STEPS, 8)),
            pltpu.SemaphoreType.DMA((n,)),
            pltpu.SemaphoreType.DMA((n,)),
        ],
        compiler_params=pltpu.CompilerParams(
            collective_id=0, has_side_effects=True, vmem_limit_bytes=48 * 1024 * 1024
        ),
        name="window",
    )(*[pltpu.with_memory_space_constraint(a, pltpu.HBM) for a in (*args[:13], traces, *positions)], segment_start)


def solution(mesh):
    block, cell = P(("shot", "gx"), "gy", None), P("gx", "gy", None)
    return jax.shard_map(
        per_device,
        mesh=mesh,
        in_specs=(block,) * 8 + (cell,) * 5 + (P("shot", ("gx", "gy")), P(), P(), P()),
        out_specs=(block,) * 3,
        check_vma=False,
    )
```

```python
import functools

import jax
import jax.numpy as jnp
from jax import lax
from jax.experimental import pallas as pl
from jax.experimental.pallas import tpu as pltpu
from jax.sharding import PartitionSpec as P

STEPS = 4
REC_DEPTH = 4
TOP = 8
LANES = 128
DIRS = tuple((dx, dy) for dx in (-1, 0, 1) for dy in (-1, 0, 1) if (dx, dy) != (0, 0))
DIRS = tuple(sorted(DIRS, key=lambda d: abs(d[0]) + abs(d[1])))
MESH = pl.DeviceIdType.MESH


def sine(x):
    s = x * x
    c = 1.6059044e-10
    for k in (-2.5052108e-8, 2.7557319e-6, -1.98412698e-4, 8.3333333e-3, -1.66666667e-1):
        c = c * s + k
    return x + x * (s * c)


def cosine(x):
    s = x * x
    c = -1.1470746e-11
    for k in (2.0876757e-9, -2.7557319e-7, 2.4801587e-5, -1.38888889e-3, 4.16666667e-2, -0.5):
        c = c * s + k
    return 1.0 + s * c


def kernel(sizes, *refs):
    n_gx, n_gy, nx, ny, nz, local_rec, n_rec = sizes
    fields, model = refs[:8], refs[8:13]
    traces, rec_x, rec_y, start = refs[13:17]
    image, p_last, q_last = refs[17:20]
    (*held, olds, coef, earth, inject, rows, window, gathered, rec_pos,
     load_sem, send_sem, recv_sem, far_send, far_recv) = refs[20:]
    waves = (held[:STEPS + 1], held[STEPS + 1:])
    n = n_gx * n_gy
    gx, gy = lax.axis_index("gx"), lax.axis_index("gy")
    me = gx * n_gy + gy

    barrier = pltpu.get_barrier_semaphore()

    def peer_id(i):
        peer = lax.rem(me + i, n)
        return {"gx": peer // n_gy, "gy": lax.rem(peer, n_gy)}

    def greet(i, carry):
        pl.semaphore_signal(barrier, inc=1, device_id=peer_id(i), device_id_type=MESH)
        return carry

    lax.fori_loop(1, n, greet, 0)

    inner_x, inner_y = pl.ds(1, nx), pl.ds(TOP, ny)
    loads = {}

    def load(name, src, dst):
        copy = pltpu.make_async_copy(src, dst, load_sem.at[len(loads)])
        copy.start()
        loads[name] = copy

    load("traces", traces, rows)
    for g in range(2):
        for f in range(2):
            load(("now", g, f), fields[4 * g + 2 * f + 1], waves[g][0].at[f, inner_x, inner_y])
    for i in range(5):
        load(("model", i), model[i], earth.at[i])
    for g in range(2):
        for f in range(2):
            load(("prev", g, f), fields[4 * g + 2 * f], olds.at[g, f])
    load("rx", rec_x, rec_pos.at[0])
    load("ry", rec_y, rec_pos.at[1])

    for edge, plane in ((gx == 0, 0), (gx == n_gx - 1, nx + 1)):
        @pl.when(edge)
        def _():
            for g in range(2):
                for level in range(STEPS):
                    for f in range(2):
                        waves[g][level][f, plane, TOP - 8:TOP + ny + 8] = jnp.zeros((ny + 16, nz), jnp.float32)
    for edge, row in ((gy == 0, TOP - 1), (gy == n_gy - 1, TOP + ny)):
        @pl.when(edge)
        def _():
            for g in range(2):
                for level in range(STEPS):
                    for f in range(2):
                        waves[g][level][f, :, row:row + 1] = jnp.zeros((nx + 2, 1, nz), jnp.float32)

    loads["traces"].wait()
    window[...] = jnp.zeros_like(window)
    window[0:STEPS, 0:local_rec] = rows[pl.ds(start[0], STEPS), :]

    def there(dx, dy):
        ok = None
        for d, pos, count in ((dx, gx, n_gx), (dy, gy, n_gy)):
            if d:
                test = pos + d < count if d > 0 else pos + d >= 0
                ok = test if ok is None else ok & test
        return ok

    def halo_copy(g, level, i):
        dx, dy = DIRS[i]
        src_x = {0: inner_x, 1: pl.ds(nx, 1), -1: pl.ds(1, 1)}[dx]
        dst_x = {0: inner_x, 1: pl.ds(0, 1), -1: pl.ds(nx + 1, 1)}[dx]
        src_y = {0: inner_y, 1: pl.ds(TOP + ny - 1, 1), -1: pl.ds(TOP, 1)}[dy]
        dst_y = {0: inner_y, 1: pl.ds(TOP - 1, 1), -1: pl.ds(TOP + ny, 1)}[dy]
        return pltpu.make_async_remote_copy(
            src_ref=waves[g][level].at[:, src_x, src_y],
            dst_ref=waves[g][level].at[:, dst_x, dst_y],
            send_sem=send_sem.at[g, level, i],
            recv_sem=recv_sem.at[g, level, i],
            device_id={"gx": gx + dx, "gy": gy + dy},
            device_id_type=MESH,
        )

    def send_halo(g, level):
        for i, (dx, dy) in enumerate(DIRS):
            @pl.when(there(dx, dy))
            def _():
                halo_copy(g, level, i).start()

    def await_halo(g, level):
        for i, (dx, dy) in enumerate(DIRS):
            @pl.when(there(-dx, -dy))
            def _():
                halo_copy(g, level, i).wait_recv()

    def finish_halo(g, level):
        for i, (dx, dy) in enumerate(DIRS):
            @pl.when(there(dx, dy))
            def _():
                halo_copy(g, level, i).wait_send()

    def far_copy(i):
        return pltpu.make_async_remote_copy(
            src_ref=window,
            dst_ref=gathered.at[me],
            send_sem=far_send.at[i],
            recv_sem=far_recv.at[me],
            device_id=peer_id(i),
            device_id_type=MESH,
        )

    def far_start(i, carry):
        far_copy(i).start()
        return carry

    def far_finish(i, carry):
        far_copy(i).wait_send()
        return carry

    def far_await(i, carry):
        peer = lax.rem(me + i, n)
        pltpu.make_async_remote_copy(
            src_ref=window,
            dst_ref=gathered.at[peer],
            send_sem=far_send.at[i],
            recv_sem=far_recv.at[peer],
            device_id=peer_id(i),
            device_id_type=MESH,
        ).wait_recv()
        return carry

    for g in range(2):
        for f in range(2):
            loads["now", g, f].wait()
    gathered[me] = window[...]
    pl.semaphore_wait(barrier, n - 1)
    send_halo(0, 0)
    lax.fori_loop(1, n, far_start, 0)
    send_halo(1, 0)

    for i in range(5):
        loads["model", i].wait()

    lane = lax.broadcasted_iota(jnp.int32, (ny, nz), 1)
    first, last = lane == 0, lane == nz - 1

    def after(value):
        return pltpu.roll(value, nz - 1, 1)

    def before(value):
        return pltpu.roll(value, 1, 1)

    def factors(x, carry):
        v = earth[0, x]
        f_e = 1.0 + 2.0 * earth[1, x]
        f_d = jnp.sqrt(1.0 + 2.0 * earth[2, x])
        tilt = earth[3, x]
        half = 0.5 * earth[4, x]
        sin_t, cos_t = sine(tilt), cosine(tilt)
        sin_h, cos_h = sine(half), cosine(half)
        sin_a = 2.0 * sin_h * cos_h
        cos_a = 1.0 - 2.0 * sin_h * sin_h
        square = sin_t * sin_t
        twice = (0.5 * sin_t) * cos_t
        a_xx = square * cos_a * cos_a
        a_yy = square * sin_a * sin_a
        a_zz = cos_t * cos_t
        a_xz, a_yz = twice * cos_a, twice * sin_a
        coef[0, x] = a_xx
        coef[1, x] = a_yy
        coef[4, x] = 1.0 - a_xx
        coef[5, x] = 1.0 - a_yy
        coef[8, x] = (0.5 * square) * sin_a * cos_a
        for shift, edge, i in ((before, first, 0), (after, last, 1)):
            moved = shift(a_zz)
            coef[2 + i, x] = jnp.where(edge, 0.0, moved)
            coef[6 + i, x] = jnp.where(edge, 0.0, 1.0 - moved)
            coef[9 + 2 * i, x] = jnp.where(edge, 0.0, shift(a_xz))
            coef[10 + 2 * i, x] = jnp.where(edge, 0.0, shift(a_yz))
        coef[13, x] = v * f_e
        coef[14, x] = v * f_d
        return carry

    lax.fori_loop(0, nx, factors, 0, unroll=4)

    for g in range(2):
        for f in range(2):
            loads["prev", g, f].wait()
    loads["rx"].wait()
    loads["ry"].wait()

    mid, up, down = pl.ds(TOP, ny), pl.ds(TOP + 1, ny), pl.ds(TOP - 1, ny)

    def rotated(now, f, x, center, weights):
        sign, w_x, w_y, w_up, w_down = weights
        x_up, x_down = now[f, x + 2, mid], now[f, x, mid]
        y_up, y_down = now[f, x + 1, up], now[f, x + 1, down]
        d_x, d_y = x_up - x_down, y_up - y_down
        d_xy = (now[f, x + 2, up] - now[f, x + 2, down]) - (now[f, x, up] - now[f, x, down])
        flat = coef[w_x, x] * (x_up + x_down) + coef[w_y, x] * (y_up + y_down)
        mixed = coef[8, x] * d_xy
        above, below = coef[w_up, x] * center, coef[w_down, x] * center
        mixed_above = coef[9, x] * d_x + coef[10, x] * d_y
        mixed_below = coef[11, x] * d_x + coef[12, x] * d_y
        if sign > 0:
            return (flat + mixed) + (after(above + mixed_above) + before(below - mixed_below))
        return (flat - mixed) + (after(above - mixed_above) + before(below + mixed_below))

    def step(g, level):
        now = waves[g][level]

        def plane(x, carry):
            p_now, q_now = now[0, x + 1, mid], now[1, x + 1, mid]
            p_two, q_two = p_now + p_now, q_now + q_now
            across = rotated(now, 0, x, p_now, (-1, 4, 5, 6, 7)) - (p_two + p_two)
            q_axis = rotated(now, 1, x, q_now, (1, 0, 1, 2, 3)) - q_two
            if level == 0:
                p_prev, q_prev = olds[g, 0, x], olds[g, 1, x]
            else:
                p_prev, q_prev = waves[g][level - 1][0, x + 1, mid], waves[g][level - 1][1, x + 1, mid]
            v_d = coef[14, x]
            p_next = (p_two - p_prev) + (coef[13, x] * across + v_d * q_axis)
            q_next = (q_two - q_prev) + (v_d * across + earth[0, x] * q_axis)
            if g == 1:
                p_next = p_next + inject[STEPS - 1 - level, x]
            if g == 1 and level == STEPS - 1:
                p_last[x] = p_next
                q_last[x] = q_next
                total = waves[0][0][0, x + 1, mid] * p_next
                for k in range(STEPS):
                    total = total + waves[1][k][0, x + 1, mid] * waves[0][STEPS - k][0, x + 1, mid]
                image[x] = total
            else:
                waves[g][level + 1][0, x + 1, mid] = p_next
                waves[g][level + 1][1, x + 1, mid] = q_next
            return carry

        lax.fori_loop(0, nx, plane, 0, unroll=8)

    def make_planes():
        per_row = LANES // local_rec
        n_rows = n_rec // LANES
        chunk = min(8, n_rows)
        x_id = lax.broadcasted_iota(jnp.int32, (nx, LANES), 0) + gx * nx
        y_id = lax.broadcasted_iota(jnp.int32, (ny, LANES), 0) + gy * ny
        total = jnp.zeros((ny, STEPS * nx), jnp.float32)
        for base in range(0, n_rows, chunk):
            lefts, rights = [], []
            for i in range(base, base + chunk):
                sample = gathered[i * per_row]
                for j in range(1, per_row):
                    sample = sample + pltpu.roll(gathered[i * per_row + j], j * local_rec, 1)
                at_x = rec_pos[0, i:i + 1] == x_id
                lefts.append(jnp.where(rec_pos[1, i:i + 1] == y_id, 1.0, 0.0))
                rights.append(
                    jnp.concatenate(
                        [jnp.where(at_x, sample[k:k + 1], 0.0) for k in range(STEPS)], axis=0
                    )
                )
            total = total + lax.dot_general(
                jnp.concatenate(lefts, axis=1),
                jnp.concatenate(rights, axis=1),
                (((1,), (1,)), ((), ())),
                precision=lax.Precision.HIGHEST,
                preferred_element_type=jnp.float32,
            )
        here = lane == REC_DEPTH
        for k in range(STEPS):
            for x in range(nx):
                column = k * nx + x
                inject[k, x] = jnp.where(here, total[:, column:column + 1], 0.0)

    for level in range(STEPS):
        await_halo(0, level)
        step(0, level)
        if level < STEPS - 1:
            send_halo(0, level + 1)
        if level == 0:
            lax.fori_loop(1, n, far_await, 0)
            make_planes()
        await_halo(1, level)
        step(1, level)
        if level < STEPS - 1:
            send_halo(1, level + 1)
    lax.fori_loop(1, n, far_finish, 0)
    for level in range(STEPS):
        for g in range(2):
            finish_halo(g, level)


def per_device(*args):
    nx, ny, nz = args[0].shape
    n_gx, n_gy = lax.axis_size("gx"), lax.axis_size("gy")
    traces, receiver_x, receiver_y, segment_start = args[13:]
    samples, local_rec = traces.shape
    n_rec = receiver_x.shape[0]
    n = n_gx * n_gy
    sizes = (n_gx, n_gy, nx, ny, nz, local_rec, n_rec)
    positions = [r.reshape(n_rec // LANES, LANES) for r in (receiver_x, receiver_y)]
    anywhere = pl.BlockSpec(memory_space=pltpu.HBM)
    block = jax.ShapeDtypeStruct((nx, ny, nz), jnp.float32)
    return pl.pallas_call(
        functools.partial(kernel, sizes),
        out_shape=(block,) * 3,
        in_specs=[anywhere] * 16 + [pl.BlockSpec(memory_space=pltpu.SMEM)],
        out_specs=(pl.BlockSpec(memory_space=pltpu.VMEM),) * 3,
        scratch_shapes=[
            *[pltpu.VMEM((2, nx + 2, ny + 16, nz), jnp.float32)] * (2 * STEPS + 2),
            pltpu.VMEM((2, 2, nx, ny, nz), jnp.float32),
            pltpu.VMEM((15, nx, ny, nz), jnp.float32),
            pltpu.VMEM((5, nx, ny, nz), jnp.float32),
            pltpu.VMEM((STEPS, nx, ny, nz), jnp.float32),
            pltpu.VMEM((samples, local_rec), jnp.float32),
            pltpu.VMEM((8, LANES), jnp.float32),
            pltpu.VMEM((n, 8, LANES), jnp.float32),
            pltpu.VMEM((2, n_rec // LANES, LANES), jnp.int32),
            pltpu.SemaphoreType.DMA((16,)),
            pltpu.SemaphoreType.DMA((2, STEPS, 8)),
            pltpu.SemaphoreType.DMA((2, STEPS, 8)),
            pltpu.SemaphoreType.DMA((n,)),
            pltpu.SemaphoreType.DMA((n,)),
        ],
        compiler_params=pltpu.CompilerParams(
            collective_id=0, has_side_effects=True, vmem_limit_bytes=48 * 1024 * 1024
        ),
        name="window",
    )(*[pltpu.with_memory_space_constraint(a, pltpu.HBM) for a in (*args[:13], traces, *positions)], segment_start)


def solution(mesh):
    block, cell = P(("shot", "gx"), "gy", None), P("gx", "gy", None)
    return jax.shard_map(
        per_device,
        mesh=mesh,
        in_specs=(block,) * 8 + (cell,) * 5 + (P("shot", ("gx", "gy")), P(), P(), P()),
        out_specs=(block,) * 3,
        check_vma=False,
    )
```

```python
import functools

import jax
import jax.numpy as jnp
from jax import lax
from jax.experimental import pallas as pl
from jax.experimental.pallas import tpu as pltpu
from jax.sharding import PartitionSpec as P

STEPS = 4
REC_DEPTH = 4
TOP = 8
LANES = 128
DIRS = tuple((dx, dy) for dx in (-1, 0, 1) for dy in (-1, 0, 1) if (dx, dy) != (0, 0))
DIRS = tuple(sorted(DIRS, key=lambda d: (abs(d[0]) + abs(d[1]), abs(d[0]))))
MESH = pl.DeviceIdType.MESH


def sine(x):
    s = x * x
    c = 1.6059044e-10
    for k in (-2.5052108e-8, 2.7557319e-6, -1.98412698e-4, 8.3333333e-3, -1.66666667e-1):
        c = c * s + k
    return x + x * (s * c)


def cosine(x):
    s = x * x
    c = -1.1470746e-11
    for k in (2.0876757e-9, -2.7557319e-7, 2.4801587e-5, -1.38888889e-3, 4.16666667e-2, -0.5):
        c = c * s + k
    return 1.0 + s * c


def kernel(sizes, *refs):
    n_gx, n_gy, nx, ny, nz, local_rec, n_rec = sizes
    fields, model = refs[:8], refs[8:13]
    traces, rec_x, rec_y, start = refs[13:17]
    image, p_last, q_last = refs[17:20]
    (*held, olds, coef, earth, inject, rows, window, gathered, rec_pos,
     load_sem, send_sem, recv_sem, far_send, far_recv) = refs[20:]
    waves = (held[:STEPS + 1], held[STEPS + 1:])
    n = n_gx * n_gy
    gx, gy = lax.axis_index("gx"), lax.axis_index("gy")
    me = gx * n_gy + gy

    barrier = pltpu.get_barrier_semaphore()

    def peer_id(i):
        peer = lax.rem(me + i, n)
        return {"gx": peer // n_gy, "gy": lax.rem(peer, n_gy)}

    def greet(i, carry):
        pl.semaphore_signal(barrier, inc=1, device_id=peer_id(i), device_id_type=MESH)
        return carry

    lax.fori_loop(1, n, greet, 0)

    inner_x, inner_y = pl.ds(1, nx), pl.ds(TOP, ny)
    loads = {}

    def load(name, src, dst):
        copy = pltpu.make_async_copy(src, dst, load_sem.at[len(loads)])
        copy.start()
        loads[name] = copy

    load("traces", traces, rows)
    for g in range(2):
        for f in range(2):
            load(("now", g, f), fields[4 * g + 2 * f + 1], waves[g][0].at[f, inner_x, inner_y])
    for i in range(5):
        load(("model", i), model[i], earth.at[i])
    for g in range(2):
        for f in range(2):
            load(("prev", g, f), fields[4 * g + 2 * f], olds.at[g, f])
    load("rx", rec_x, rec_pos.at[0])
    load("ry", rec_y, rec_pos.at[1])

    for edge, plane in ((gx == 0, 0), (gx == n_gx - 1, nx + 1)):
        @pl.when(edge)
        def _():
            for g in range(2):
                for level in range(STEPS):
                    for f in range(2):
                        waves[g][level][f, plane, TOP - 8:TOP + ny + 8] = jnp.zeros((ny + 16, nz), jnp.float32)
    for edge, row in ((gy == 0, TOP - 1), (gy == n_gy - 1, TOP + ny)):
        @pl.when(edge)
        def _():
            for g in range(2):
                for level in range(STEPS):
                    for f in range(2):
                        waves[g][level][f, :, row:row + 1] = jnp.zeros((nx + 2, 1, nz), jnp.float32)

    loads["traces"].wait()
    window[...] = jnp.zeros_like(window)
    window[0:STEPS, 0:local_rec] = rows[pl.ds(start[0], STEPS), :]

    def there(dx, dy):
        ok = None
        for d, pos, count in ((dx, gx, n_gx), (dy, gy, n_gy)):
            if d:
                test = pos + d < count if d > 0 else pos + d >= 0
                ok = test if ok is None else ok & test
        return ok

    def halo_copy(g, level, i):
        dx, dy = DIRS[i]
        src_x = {0: inner_x, 1: pl.ds(nx, 1), -1: pl.ds(1, 1)}[dx]
        dst_x = {0: inner_x, 1: pl.ds(0, 1), -1: pl.ds(nx + 1, 1)}[dx]
        src_y = {0: inner_y, 1: pl.ds(TOP + ny - 1, 1), -1: pl.ds(TOP, 1)}[dy]
        dst_y = {0: inner_y, 1: pl.ds(TOP - 1, 1), -1: pl.ds(TOP + ny, 1)}[dy]
        return pltpu.make_async_remote_copy(
            src_ref=waves[g][level].at[:, src_x, src_y],
            dst_ref=waves[g][level].at[:, dst_x, dst_y],
            send_sem=send_sem.at[g, level, i],
            recv_sem=recv_sem.at[g, level, i],
            device_id={"gx": gx + dx, "gy": gy + dy},
            device_id_type=MESH,
        )

    def send_halo(g, level):
        for i, (dx, dy) in enumerate(DIRS):
            @pl.when(there(dx, dy))
            def _():
                halo_copy(g, level, i).start()

    def await_halo(g, level):
        for i, (dx, dy) in enumerate(DIRS):
            @pl.when(there(-dx, -dy))
            def _():
                halo_copy(g, level, i).wait_recv()

    def finish_halo(g, level):
        for i, (dx, dy) in enumerate(DIRS):
            @pl.when(there(dx, dy))
            def _():
                halo_copy(g, level, i).wait_send()

    def far_copy(i):
        return pltpu.make_async_remote_copy(
            src_ref=window,
            dst_ref=gathered.at[me],
            send_sem=far_send.at[i],
            recv_sem=far_recv.at[me],
            device_id=peer_id(i),
            device_id_type=MESH,
        )

    def far_start(i, carry):
        far_copy(i).start()
        return carry

    def far_finish(i, carry):
        far_copy(i).wait_send()
        return carry

    def far_await(i, carry):
        peer = lax.rem(me + i, n)
        pltpu.make_async_remote_copy(
            src_ref=window,
            dst_ref=gathered.at[peer],
            send_sem=far_send.at[i],
            recv_sem=far_recv.at[peer],
            device_id=peer_id(i),
            device_id_type=MESH,
        ).wait_recv()
        return carry

    gathered[me] = window[...]
    pl.semaphore_wait(barrier, n - 1)
    for g in range(2):
        for f in range(2):
            loads["now", g, f].wait()
    lax.fori_loop(1, n, far_start, 0)
    send_halo(0, 0)
    send_halo(1, 0)

    for i in range(5):
        loads["model", i].wait()

    lane = lax.broadcasted_iota(jnp.int32, (ny, nz), 1)
    first, last = lane == 0, lane == nz - 1

    def after(value):
        return pltpu.roll(value, nz - 1, 1)

    def before(value):
        return pltpu.roll(value, 1, 1)

    def factors(x, carry):
        v = earth[0, x]
        f_e = 1.0 + 2.0 * earth[1, x]
        f_d = jnp.sqrt(1.0 + 2.0 * earth[2, x])
        tilt = earth[3, x]
        half = 0.5 * earth[4, x]
        sin_t, cos_t = sine(tilt), cosine(tilt)
        sin_h, cos_h = sine(half), cosine(half)
        sin_a = 2.0 * sin_h * cos_h
        cos_a = 1.0 - 2.0 * sin_h * sin_h
        square = sin_t * sin_t
        twice = (0.5 * sin_t) * cos_t
        a_xx = square * cos_a * cos_a
        a_yy = square * sin_a * sin_a
        a_zz = cos_t * cos_t
        a_xz, a_yz = twice * cos_a, twice * sin_a
        coef[0, x] = a_xx
        coef[1, x] = a_yy
        coef[4, x] = 1.0 - a_xx
        coef[5, x] = 1.0 - a_yy
        coef[8, x] = (0.5 * square) * sin_a * cos_a
        for shift, edge, i in ((before, first, 0), (after, last, 1)):
            moved = shift(a_zz)
            coef[2 + i, x] = jnp.where(edge, 0.0, moved)
            coef[6 + i, x] = jnp.where(edge, 0.0, 1.0 - moved)
            coef[9 + 2 * i, x] = jnp.where(edge, 0.0, shift(a_xz))
            coef[10 + 2 * i, x] = jnp.where(edge, 0.0, shift(a_yz))
        coef[13, x] = v * f_e
        coef[14, x] = v * f_d
        return carry

    lax.fori_loop(0, nx, factors, 0, unroll=4)

    for g in range(2):
        for f in range(2):
            loads["prev", g, f].wait()
    loads["rx"].wait()
    loads["ry"].wait()

    mid, up, down = pl.ds(TOP, ny), pl.ds(TOP + 1, ny), pl.ds(TOP - 1, ny)

    def rotated(now, f, x, center, weights):
        sign, w_x, w_y, w_up, w_down = weights
        x_up, x_down = now[f, x + 2, mid], now[f, x, mid]
        y_up, y_down = now[f, x + 1, up], now[f, x + 1, down]
        d_x, d_y = x_up - x_down, y_up - y_down
        d_xy = (now[f, x + 2, up] - now[f, x + 2, down]) - (now[f, x, up] - now[f, x, down])
        flat = coef[w_x, x] * (x_up + x_down) + coef[w_y, x] * (y_up + y_down)
        mixed = coef[8, x] * d_xy
        above, below = coef[w_up, x] * center, coef[w_down, x] * center
        mixed_above = coef[9, x] * d_x + coef[10, x] * d_y
        mixed_below = coef[11, x] * d_x + coef[12, x] * d_y
        if sign > 0:
            return (flat + mixed) + (after(above + mixed_above) + before(below - mixed_below))
        return (flat - mixed) + (after(above - mixed_above) + before(below + mixed_below))

    def step(g, level):
        now = waves[g][level]

        def plane(x, carry):
            p_now, q_now = now[0, x + 1, mid], now[1, x + 1, mid]
            p_two, q_two = p_now + p_now, q_now + q_now
            across = rotated(now, 0, x, p_now, (-1, 4, 5, 6, 7)) - (p_two + p_two)
            q_axis = rotated(now, 1, x, q_now, (1, 0, 1, 2, 3)) - q_two
            if level == 0:
                p_prev, q_prev = olds[g, 0, x], olds[g, 1, x]
            else:
                p_prev, q_prev = waves[g][level - 1][0, x + 1, mid], waves[g][level - 1][1, x + 1, mid]
            v_d = coef[14, x]
            p_next = (p_two - p_prev) + (coef[13, x] * across + v_d * q_axis)
            q_next = (q_two - q_prev) + (v_d * across + earth[0, x] * q_axis)
            if g == 1:
                p_next = p_next + inject[STEPS - 1 - level, x]
            if g == 1 and level == STEPS - 1:
                p_last[x] = p_next
                q_last[x] = q_next
                total = waves[0][0][0, x + 1, mid] * p_next
                for k in range(STEPS):
                    total = total + waves[1][k][0, x + 1, mid] * waves[0][STEPS - k][0, x + 1, mid]
                image[x] = total
            else:
                waves[g][level + 1][0, x + 1, mid] = p_next
                waves[g][level + 1][1, x + 1, mid] = q_next
            return carry

        lax.fori_loop(0, nx, plane, 0, unroll=8)

    def make_planes():
        per_row = LANES // local_rec
        n_rows = n_rec // LANES
        chunk = min(8, n_rows)
        x_id = lax.broadcasted_iota(jnp.int32, (nx, LANES), 0) + gx * nx
        y_id = lax.broadcasted_iota(jnp.int32, (ny, LANES), 0) + gy * ny
        total = jnp.zeros((ny, STEPS * nx), jnp.float32)
        for base in range(0, n_rows, chunk):
            lefts, rights = [], []
            for i in range(base, base + chunk):
                sample = gathered[i * per_row]
                for j in range(1, per_row):
                    sample = sample + pltpu.roll(gathered[i * per_row + j], j * local_rec, 1)
                at_x = rec_pos[0, i:i + 1] == x_id
                lefts.append(jnp.where(rec_pos[1, i:i + 1] == y_id, 1.0, 0.0))
                rights.append(
                    jnp.concatenate(
                        [jnp.where(at_x, sample[k:k + 1], 0.0) for k in range(STEPS)], axis=0
                    )
                )
            total = total + lax.dot_general(
                jnp.concatenate(lefts, axis=1),
                jnp.concatenate(rights, axis=1),
                (((1,), (1,)), ((), ())),
                precision=lax.Precision.HIGHEST,
                preferred_element_type=jnp.float32,
            )
        here = lane == REC_DEPTH
        for k in range(STEPS):
            for x in range(nx):
                column = k * nx + x
                inject[k, x] = jnp.where(here, total[:, column:column + 1], 0.0)

    for level in range(STEPS):
        await_halo(0, level)
        step(0, level)
        if level < STEPS - 1:
            send_halo(0, level + 1)
        if level == 0:
            lax.fori_loop(1, n, far_await, 0)
            make_planes()
        await_halo(1, level)
        step(1, level)
        if level < STEPS - 1:
            send_halo(1, level + 1)
    lax.fori_loop(1, n, far_finish, 0)
    for level in range(STEPS):
        for g in range(2):
            finish_halo(g, level)


def write_out(*refs):
    values, results, done = refs[:3], refs[3:6], refs[6]
    copies = [pltpu.make_async_copy(values[i], results[i], done.at[i]) for i in range(3)]
    for copy in copies:
        copy.start()
    for copy in copies:
        copy.wait()


def per_device(*args):
    nx, ny, nz = args[0].shape
    n_gx, n_gy = lax.axis_size("gx"), lax.axis_size("gy")
    traces, receiver_x, receiver_y, segment_start = args[13:]
    samples, local_rec = traces.shape
    n_rec = receiver_x.shape[0]
    n = n_gx * n_gy
    sizes = (n_gx, n_gy, nx, ny, nz, local_rec, n_rec)
    positions = [r.reshape(n_rec // LANES, LANES) for r in (receiver_x, receiver_y)]
    anywhere = pl.BlockSpec(memory_space=pltpu.HBM)
    block = jax.ShapeDtypeStruct((nx, ny, nz), jnp.float32)
    held = pltpu.VMEM((nx, ny, nz), jnp.float32)
    ends = pl.pallas_call(
        functools.partial(kernel, sizes),
        out_shape=(held,) * 3,
        in_specs=[anywhere] * 16 + [pl.BlockSpec(memory_space=pltpu.SMEM)],
        out_specs=(pl.BlockSpec(memory_space=pltpu.VMEM),) * 3,
        scratch_shapes=[
            *[pltpu.VMEM((2, nx + 2, ny + 16, nz), jnp.float32)] * (2 * STEPS + 2),
            pltpu.VMEM((2, 2, nx, ny, nz), jnp.float32),
            pltpu.VMEM((15, nx, ny, nz), jnp.float32),
            pltpu.VMEM((5, nx, ny, nz), jnp.float32),
            pltpu.VMEM((STEPS, nx, ny, nz), jnp.float32),
            pltpu.VMEM((samples, local_rec), jnp.float32),
            pltpu.VMEM((8, LANES), jnp.float32),
            pltpu.VMEM((n, 8, LANES), jnp.float32),
            pltpu.VMEM((2, n_rec // LANES, LANES), jnp.int32),
            pltpu.SemaphoreType.DMA((16,)),
            pltpu.SemaphoreType.DMA((2, STEPS, 8)),
            pltpu.SemaphoreType.DMA((2, STEPS, 8)),
            pltpu.SemaphoreType.DMA((n,)),
            pltpu.SemaphoreType.DMA((n,)),
        ],
        compiler_params=pltpu.CompilerParams(
            collective_id=0, has_side_effects=True, vmem_limit_bytes=48 * 1024 * 1024
        ),
        name="window",
    )(*[pltpu.with_memory_space_constraint(a, pltpu.HBM) for a in (*args[:13], traces, *positions)], segment_start)
    return pl.pallas_call(
        write_out,
        out_shape=(block,) * 3,
        in_specs=[pl.BlockSpec(memory_space=pltpu.VMEM)] * 3,
        out_specs=(pl.BlockSpec(memory_space=pltpu.HBM),) * 3,
        scratch_shapes=[pltpu.SemaphoreType.DMA((3,))],
        compiler_params=pltpu.CompilerParams(vmem_limit_bytes=1024 * 1024),
        name="write_out",
    )(*[pltpu.with_memory_space_constraint(end, pltpu.VMEM) for end in ends])


def solution(mesh):
    block, cell = P(("shot", "gx"), "gy", None), P("gx", "gy", None)
    return jax.shard_map(
        per_device,
        mesh=mesh,
        in_specs=(block,) * 8 + (cell,) * 5 + (P("shot", ("gx", "gy")), P(), P(), P()),
        out_specs=(block,) * 3,
        check_vma=False,
    )
```
